256 devices in a mesh: seq: 32 (over y_lo, z, core), vocab: 8 (over x, y_hi).
Axes of the slice: x: 4, y: 4 (y_hi: 2, y_lo: 2; y = y_hi * 2 + y_lo), z: 8, core: 2. Of those that a mesh axis runs over, the one named last changes fastest.
Arguments:
- hidden: bfloat16 [2048, 5376], P('seq'), may hold values from -40 to 40
- weight: bfloat16 [5376, 262144], P(None, ('seq', 'vocab')), may hold values from -3 to 3
- targets: int32 [2048], P('seq'), may hold values from 0 to 262143
- offsets: int32 [32], P('seq'), may hold values from 0 to 32
- counts: int32 [32], P('seq'), may hold values from 1 to 32, as said below
Outputs:
- log_prob: float32 [1024], P('seq')
The draws below stay inside these ranges and needn't reach their ends.
Inputs may be any that keep to these rules, and one draw needn't show every extreme that they name: Shard s scores rows offsets[s] to offsets[s] + counts[s] - 1 of its 64; some shard scores 32 in every draw.
All inputs are finite; a program needn't handle non-finite values.
Results may differ from the reference program's by a relative error of at most 0.0003.
Values may be sent and summed in bfloat16 or wider, within the bound.
No kernel may reach another device: no remote copies, remote signals or barrier semaphores. Data moves between devices by JAX's collectives and lax.ppermute only.
A program may use at most 64 MiB of HBM per device.

```python
import math
import jax
import jax.numpy as jnp
from jax import lax

D = 5376
SMAX = 32
VOCAB = 262144
RPS = 64
ROWS = 2048
N_SEQ = 32


def column_draw(key, column_index):
    noise = jax.random.normal(jax.random.fold_in(jax.random.fold_in(key, 7), column_index), (D,), jnp.float32)
    return jnp.clip(noise, -6.0, 6.0) * (3.0 / math.sqrt(D))


def draw_weight(key, part):
    columns = jax.vmap(lambda index: column_draw(key, index))(jnp.arange(VOCAB, dtype=jnp.int32))
    return columns.T.astype(jnp.bfloat16)


def draw_hidden(key, part):
    drawn = jax.random.normal(jax.random.fold_in(key, 1), (ROWS, D), jnp.float32)
    return jnp.clip(drawn, -6.0, 6.0).astype(jnp.bfloat16)


def draw_counts(key, part):
    values = jax.random.randint(key, (N_SEQ,), 1, SMAX + 1)
    fullest = jax.random.randint(jax.random.fold_in(key, 3), (), 0, N_SEQ)
    return values.at[fullest].set(SMAX).astype(jnp.int32)


def plant(entries, own_key, low, top_value):
    extent = entries.shape
    place = [jax.random.randint(jax.random.fold_in(own_key, axis), (), 0, extent[axis]) for axis in range(len(extent))]
    entries = entries.at[tuple(place)].set(low)
    longest = extent.index(max(extent))
    place[longest] = (place[longest] + 1) % extent[longest]
    return entries.at[tuple(place)].set(top_value)


def setup_inputs(seed: int = 0) -> dict:
    streams_of = jax.random.split(jax.random.key(seed), 6)
    hidden = draw_hidden(jax.random.fold_in(streams_of[5], 71), 0)
    weight = draw_weight(jax.random.fold_in(streams_of[5], 71), 0)
    targets = plant(jax.random.randint(streams_of[2], (ROWS,), 0, VOCAB), jax.random.fold_in(streams_of[2], 1), 0, VOCAB - 1).astype(jnp.int32)
    offsets = plant(jax.random.randint(streams_of[3], (N_SEQ,), 0, RPS - SMAX + 1), jax.random.fold_in(streams_of[3], 1), 0, RPS - SMAX).astype(jnp.int32)
    counts = draw_counts(jax.random.fold_in(streams_of[5], 71), 0)
    return dict(hidden=hidden, weight=weight, targets=targets, offsets=offsets, counts=counts)


def reference(hidden, weight, targets, offsets, counts):
    def score_shard(shard_index):
        first_row = (shard_index * RPS + offsets[shard_index]).astype(jnp.int32)
        row_block = lax.dynamic_slice_in_dim(hidden, first_row, SMAX, 0)
        target_ids = lax.dynamic_slice_in_dim(targets, first_row, SMAX, 0)
        logits = jnp.dot(row_block, weight, preferred_element_type=jnp.float32)
        row_max = jnp.max(logits, axis=1)
        totals = jnp.sum(jnp.exp(logits - row_max[:, None]), axis=1)
        picked = jnp.take_along_axis(logits, target_ids[:, None], axis=1)[:, 0]
        log_value = picked - row_max - jnp.log(totals)
        slots = jnp.arange(SMAX, dtype=jnp.int32)
        return jnp.where(slots < counts[shard_index], log_value, jnp.zeros_like(log_value))

    return lax.map(score_shard, jnp.arange(N_SEQ, dtype=jnp.int32)).reshape(-1)
```

```python
import jax
import jax.numpy as jnp
from jax import lax
from jax.sharding import PartitionSpec as P

SMAX = 32
NX, NY, NZ = 4, 4, 8
PAD = 128
AXES = ("seq", "vocab")


def device_index(x, y, z, core):
    x, y, z = x % NX, y % NY, z % NZ
    return ((y % 2) * 2 * NZ + z * 2 + core) * (2 * NX) + x * 2 + y // 2


def make_perm(dy, dz, flip):
    pairs = []
    for x in range(NX):
        for y in range(NY):
            for z in range(NZ):
                for core in range(2):
                    sign = 1 - 2 * core
                    pairs.append(
                        (device_index(x, y, z, core), device_index(x, y + sign * dy, z + sign * dz, core ^ flip))
                    )
    return pairs


Z_STEP = make_perm(0, 1, 0)
Y_STEP = make_perm(1, 0, 0)
SWAP = make_perm(0, 0, 1)


def chunk_stats(rows, weight, column_base, shift):
    d_model = weight.shape[0]
    logits = jnp.dot(rows[:, :d_model], weight, preferred_element_type=jnp.float32)
    digits = rows[:, d_model : d_model + 3].astype(jnp.int32)
    ids = digits[:, 0] * 4096 + digits[:, 1] * 64 + digits[:, 2]
    top = jnp.max(logits, axis=1)
    total = jnp.sum(jnp.exp(logits - top[:, None]), axis=1)
    columns = lax.broadcasted_iota(jnp.int32, logits.shape, 1)
    hit = jnp.sum(jnp.where(columns == (ids - column_base)[:, None], logits, 0.0), axis=1)
    return jnp.stack([a.reshape(-1, SMAX) for a in (top, total, hit)], axis=1)


def body(hidden, weight, targets, offsets, counts):
    first_row = offsets[0]
    window = lax.dynamic_slice_in_dim(hidden, first_row, SMAX, 0)
    ids = lax.dynamic_slice_in_dim(targets, first_row, SMAX, 0)
    seq, voc = lax.axis_index("seq"), lax.axis_index("vocab")
    n_voc = lax.axis_size("vocab")
    column_base = (seq * n_voc + voc) * weight.shape[1]
    lane = lax.broadcasted_iota(jnp.int32, (SMAX, PAD), 1)
    ids = ids[:, None]
    digits = jnp.where(lane == 0, ids >> 12, jnp.where(lane == 1, (ids >> 6) & 63, jnp.where(lane == 2, ids & 63, 0)))
    own = jnp.concatenate([window, digits.astype(jnp.bfloat16)], axis=1)

    core, z, y_lo = seq & 1, (seq >> 1) & (NZ - 1), seq >> 4
    sign = 1 - 2 * core

    def move(a, perm):
        return lax.ppermute(a, AXES, perm)

    def shard(y_bit, hops, bit, other):
        step = -hops * sign * (1 - 2 * other)
        return (y_lo ^ y_bit) * (2 * NZ) + ((z + step) & (NZ - 1)) * 2 + (core ^ other ^ bit)

    block = jnp.concatenate([own, move(own, SWAP)], axis=0)
    side = move(own, Y_STEP)
    chunks = [([block, side, move(side, SWAP)], [shard(0, 0, 0, 0), shard(0, 0, 1, 0), shard(1, 0, 0, 0), shard(1, 0, 0, 1)])]
    for hops in range(1, NZ // 2 + 1):
        last = hops == NZ // 2
        block = move(block[:SMAX] if last else block, Z_STEP)
        side = move(block, Y_STEP)
        parts = [block, side, move(block, SWAP), move(side, SWAP)]
        bits = (0,) if last else (0, 1)
        shards = [shard(y_bit, hops, bit, other) for other in (0, 1) for y_bit in (0, 1) for bit in bits]
        chunks.append((parts, shards))

    stats, order = [], []
    for group in ((0, 1), (2,), (3,), (4,)):
        parts = [p for g in group for p in chunks[g][0]]
        order += [s for g in group for s in chunks[g][1]]
        stats.append(chunk_stats(jnp.concatenate(parts, axis=0), weight, column_base, None))
    stats = jnp.concatenate(stats, axis=0).reshape(-1, 3 * SMAX)
    n_seq = stats.shape[0]
    order = jnp.stack(order)
    place = (lax.broadcasted_iota(jnp.int32, (n_seq, n_seq), 0) == order[None, :]).astype(jnp.float32)
    by_shard = jnp.dot(place, stats, precision=lax.Precision.HIGHEST)
    outgoing = jnp.repeat(by_shard, n_voc, axis=0)
    incoming = lax.all_to_all(outgoing, AXES, 0, 0, tiled=True)
    tops, totals, hits = incoming[:, :SMAX], incoming[:, SMAX : 2 * SMAX], incoming[:, 2 * SMAX :]
    largest = jnp.max(tops, axis=0)
    total = jnp.sum(totals * jnp.exp(tops - largest[None, :]), axis=0)
    log_value = jnp.sum(hits, axis=0) - largest - jnp.log(total)
    slots = lax.broadcasted_iota(jnp.int32, (SMAX,), 0)
    return jnp.where(slots < counts[0], log_value, 0.0)


def solution(mesh):
    in_specs = (P("seq", None), P(None, ("seq", "vocab")), P("seq"), P("seq"), P("seq"))
    out_specs = P("seq")
    return jax.shard_map(body, mesh=mesh, in_specs=in_specs, out_specs=out_specs, check_vma=False)
```
